256 devices in a mesh: cols: 64 (over z, y_lo, x), par: 4 (over y_hi, core).
Axes of the slice: x: 4, y: 4 (y_hi: 2, y_lo: 2; y = y_hi * 2 + y_lo), z: 8, core: 2. Of those that a mesh axis runs over, the one named last changes fastest.
Arguments:
- tile_bounds: int32 [65], replicated, may hold values from 0 to 16384, as said below
- tile_anchor: int32 [512, 2], P(('cols', 'par')), may hold values from 0 to 256, as said below
- tile_picks: int32 [512], P(('cols', 'par')), may hold values from 16 to 64, as said below
- rmo_picks: bfloat16 [512, 64], P(('cols', 'par')), may hold values from -6 to 6
- sensitivity: bfloat16 [512, 64, 3, 16, 128], P(('cols', 'par')), may hold values from -0.75 to 0.75
- dip_class: int32 [256, 64, 256], P(('cols', 'par')), may hold values from 0 to 8
- strength: float32 [3], replicated, may hold values from 0.05 to 0.2
- couple: float32 [3, 3], replicated, may hold values from 0.1 to 1
Outputs:
- model_update: float32 [3, 256, 64, 256], P(None, ('cols', 'par'))
The draws below stay inside these ranges and needn't reach their ends.
Inputs may be any that keep to these rules, and one draw needn't show every extreme that they name: tile_bounds[0] = 0 and tile_bounds[64] = 16384; column tile c holds grid columns tile_bounds[c] to tile_bounds[c + 1] - 1, between 128 and 384 of them, and some column tile holds exactly 384. Fat-ray tile t belongs to column tile t // (2 * 4); it covers depth cells tile_anchor[t, 0] to tile_anchor[t, 0] + 15 and column slots tile_anchor[t, 1] to tile_anchor[t, 1] + 127 of that column tile, all of them among its columns and within the grid. Rays 0 to tile_picks[t] - 1 of tile t are live; some tile has 64 live rays.
All inputs are finite; a program needn't handle non-finite values.
Results may differ from the reference program's by a relative error of at most 0.0003.
Values sent between devices are 32-bit elements; how exact they have to be, the bound alone decides.
A program may use at most 192 MiB of HBM per device.

```python
import math
import jax
import jax.numpy as jnp
from jax import lax

NPARAM = 3
NT = 2
RAYS = 64
TZ = 16
TC = 128
COL_DEV = 256
LY = 256
PASSES = 6
TILES = 512
NZ = 256
NCOLUMNS = 16384
LX = 64
N_COLS = 64
N_PAR = 4


def tile_layout(key):
    keys = jax.random.split(jax.random.fold_in(key, 7), 5)
    half = N_COLS // 2
    spread = jax.random.randint(keys[0], (half,), -(COL_DEV // 2), COL_DEV // 2 + 1)
    widest = jax.random.randint(keys[1], (), 0, half)
    spread = spread.at[widest].set(COL_DEV // 2)
    side = jax.random.randint(keys[2], (half,), 0, 2) * 2 - 1
    spread = spread * side
    widths = jnp.stack([COL_DEV + spread, COL_DEV - spread], axis=1).reshape(-1)
    bounds = jnp.concatenate([jnp.zeros((1,), jnp.int32), jnp.cumsum(widths).astype(jnp.int32)])
    per_tile = TILES // N_COLS
    owner_tile = jnp.arange(TILES) // per_tile
    tile_width = widths[owner_tile]
    column_first = jax.random.randint(keys[3], (TILES,), 0, tile_width - TC + 1)
    depth_first = jax.random.randint(keys[4], (TILES,), 0, NZ - TZ + 1)
    broadest = jnp.argmax(widths).astype(jnp.int32)
    first_ray_tile = broadest * per_tile
    column_first = column_first.at[first_ray_tile].set(widths[broadest] - TC)
    column_first = column_first.at[first_ray_tile + 1].set(0)
    depth_first = depth_first.at[0].set(NZ - TZ)
    depth_first = depth_first.at[1].set(0)
    anchor = jnp.stack([depth_first, column_first], axis=1).astype(jnp.int32)
    return (bounds.astype(jnp.int32), anchor)


def draw_tile_bounds(key, part):
    return tile_layout(key)[0]


def draw_tile_anchor(key, part):
    return tile_layout(key)[1]


def draw_tile_picks(key, part):
    keys = jax.random.split(jax.random.fold_in(key, 11), 2)
    picks = jax.random.randint(keys[0], (TILES,), RAYS // 4, RAYS + 1)
    fullest = jax.random.randint(keys[1], (), 0, TILES)
    return picks.at[fullest].set(RAYS).astype(jnp.int32)


def plant(array, key, smallest, largest):
    longest = array.shape.index(max(array.shape))
    spots = []
    for shift in (0, 1):
        where = [jax.random.randint(jax.random.fold_in(key, axis), (), 0, length) for axis, length in enumerate(array.shape)]
        where[longest] = (where[longest] + shift) % array.shape[longest]
        spots.append(tuple(where))
    return array.at[spots[0]].set(smallest).at[spots[1]].set(largest)


def level_of(rng, shape, shards, least, top_value):
    factor_of = 1.0
    for position, shards_of in shards:
        draws = jax.random.uniform(jax.random.fold_in(jax.random.fold_in(rng, 6), position), (shards_of,), jnp.float32, least / len(shards), top_value / len(shards))
        factor_of = factor_of * jnp.repeat(jnp.exp(draws), shape[position] // shards_of).reshape((-1,) + (1,) * (len(shape) - 1 - position))
    return factor_of


def noise(key, dims, deviation, bound, cuts=(), held_as=jnp.bfloat16):
    factor_of = level_of(key, dims, cuts, -0.22, 0.18) if cuts else 1.0
    array = jax.random.normal(key, dims, jnp.float32) * deviation * factor_of
    return jnp.minimum(jnp.maximum(array, -bound), bound).astype(held_as)


def setup_inputs(seed: int = 0) -> dict:
    arg_keys = jax.random.split(jax.random.key(seed), 9)
    return {
        "tile_bounds": draw_tile_bounds(jax.random.fold_in(arg_keys[8], 71), 0),
        "tile_anchor": draw_tile_anchor(jax.random.fold_in(arg_keys[8], 71), 0),
        "tile_picks": draw_tile_picks(jax.random.fold_in(arg_keys[8], 71), 0),
        "rmo_picks": noise(arg_keys[3], (TILES, RAYS), 1.0, 6.0, ((0, 256),)),
        "sensitivity": noise(arg_keys[4], (TILES, RAYS, NPARAM, TZ, TC), RAYS ** -0.5, 0.75, ((0, 256),)),
        "dip_class": plant(jax.random.randint(arg_keys[5], (NZ, LX, LY), 0, 9), jax.random.fold_in(arg_keys[5], 1), 0, 8).astype(jnp.int32),
        "strength": jnp.clip(jnp.exp(jax.random.uniform(arg_keys[6], (NPARAM,), jnp.float32, math.log(0.05), math.log(0.2))), 0.05, 0.2),
        "couple": jnp.clip(jnp.exp(jax.random.uniform(arg_keys[7], (NPARAM, NPARAM), jnp.float32, math.log(0.1), math.log(1.0))), 0.1, 1.0),
    }


def next_cells(values, along_dim):
    count = values.shape[along_dim]
    kept = lax.slice_in_dim(values, 1, count, axis=along_dim)
    zeros = jnp.zeros_like(lax.slice_in_dim(values, 0, 1, axis=along_dim))
    return jnp.concatenate([kept, zeros], axis=along_dim)


def prev_cells(values, along_dim):
    count = values.shape[along_dim]
    kept = lax.slice_in_dim(values, 0, count - 1, axis=along_dim)
    zeros = jnp.zeros_like(lax.slice_in_dim(values, 0, 1, axis=along_dim))
    return jnp.concatenate([zeros, kept], axis=along_dim)


def at_depth(padded, tilt):
    return jnp.where(tilt < 0, padded[:, :-2], jnp.where(tilt > 0, padded[:, 2:], padded[:, 1:-1]))


def smooth_pass(padded, dip_class, strength, mixing):
    centre = padded[:, 1:-1]
    tilt_across = (dip_class // 3 - 1)[None]
    tilt_along = (dip_class % 3 - 1)[None]
    east_side = at_depth(next_cells(padded, 2), tilt_across)
    west_side = at_depth(prev_cells(padded, 2), -tilt_across)
    north_side = at_depth(next_cells(padded, 3), tilt_along)
    south_side = at_depth(prev_cells(padded, 3), -tilt_along)
    laplace = east_side + west_side + north_side + south_side - 4.0 * centre
    smooth = centre + strength[:, None, None, None] * laplace
    return jnp.tensordot(mixing, smooth, axes=1, precision=lax.Precision.HIGHEST)


def reference(tile_bounds, tile_anchor, tile_picks, rmo_picks, sensitivity, dip_class, strength, couple):
    owner_tile = jnp.arange(TILES, dtype=jnp.int32) // (NT * N_PAR)
    column_start = (tile_bounds[owner_tile] + tile_anchor[:, 1]).astype(jnp.int32)
    depth_start = tile_anchor[:, 0].astype(jnp.int32)

    def add_tile(gradient, tile_items):
        sens_tile, rmo_tile, live_count, depth_first, column_first = tile_items
        live = jnp.arange(RAYS, dtype=jnp.int32) < live_count
        ray_weight = jnp.where(live, rmo_tile, jnp.zeros_like(rmo_tile))
        partial_value = jnp.dot(ray_weight[None, :], sens_tile.reshape(RAYS, -1), preferred_element_type=jnp.float32)
        partial_value = partial_value.reshape(NPARAM, TZ, TC).astype(gradient.dtype)
        anchor = (jnp.int32(0), depth_first, column_first)
        current = lax.dynamic_slice(gradient, anchor, (NPARAM, TZ, TC))
        return lax.dynamic_update_slice(gradient, current + partial_value, anchor), None

    gradient = jnp.zeros((NPARAM, NZ, NCOLUMNS), jnp.float32)
    gradient, _ = lax.scan(add_tile, gradient, (sensitivity, rmo_picks, tile_picks, depth_start, column_start))
    field = gradient.reshape(NPARAM, NZ, LX, LY)
    mixing = couple / jnp.sum(couple, axis=1, keepdims=True)
    for _ in range(PASSES):
        padded = jnp.pad(field, ((0, 0), (1, 1), (0, 0), (0, 0)))
        field = smooth_pass(padded, dip_class, strength, mixing)
    return field
```

```python
import functools

import jax
import jax.numpy as jnp
from jax import lax
from jax.experimental import pallas as pl
from jax.experimental.pallas import tpu as pltpu
from jax.sharding import PartitionSpec as P

CAP = 384
PASSES = 6
F32 = jnp.float32
VMEM = pl.BlockSpec(memory_space=pltpu.VMEM)
SMEM = pl.BlockSpec(memory_space=pltpu.SMEM)


def layer_of(cols, par):
    plane, y_lo, x = cols // 8, (cols // 4) % 2, cols % 4
    y_hi, core = par // 2, par % 2
    place = 4 * (2 * y_hi + y_lo) + x + y_lo * (3 - 2 * x)
    place = place + (plane % 2) * (15 - 2 * place)
    return 32 * plane + 2 * place + core


def holder_of(layer):
    plane, rest = layer // 32, layer % 32
    place, core = rest // 2, rest % 2
    place = place + (plane % 2) * (15 - 2 * place)
    y, x = place // 4, place % 4
    y_lo = y % 2
    x = x + y_lo * (3 - 2 * x)
    return 8 * plane + 4 * y_lo + x, 2 * (y // 2) + core


def to(cols, par):
    return dict(device_id={"cols": cols, "par": par}, device_id_type=pl.DeviceIdType.MESH)


def contribution_kernel(picks, rmo, sens, out):
    tiles, rays = rmo.shape
    ray = lax.broadcasted_iota(jnp.int32, (1, rays), 1)
    for t in range(tiles):
        weight = jnp.where(ray < picks[t], rmo[t : t + 1, :].astype(F32), 0.0)
        total = jnp.zeros(out.shape[1:], F32)
        for r in range(rays):
            total += weight[:, r : r + 1][None] * sens[t, r].astype(F32)
        out[t] = total


def share_kernel(anchor, mine, tiles, anchors, mine_anchor, sends, recvs, anchor_sends, anchor_recvs):
    cols, par = lax.axis_index("cols"), lax.axis_index("par")
    peers = [(par + step) % 4 for step in (1, 2, 3)]
    barrier = pltpu.get_barrier_semaphore()
    for peer in peers:
        pl.semaphore_signal(barrier, inc=1, **to(cols, peer))
    row = lax.broadcasted_iota(jnp.int32, (8, 128), 0)
    lane = lax.broadcasted_iota(jnp.int32, (8, 128), 1)
    table = jnp.zeros((8, 128), jnp.int32)
    for t in range(2):
        for k in range(2):
            table = jnp.where((row == t) & (lane == k), anchor[t, k], table)
    mine_anchor[...] = table
    anchors[par] = table
    tiles[par] = mine[...]
    pl.semaphore_wait(barrier, 3)
    copies = []
    for step, peer in enumerate(peers):
        copies.append(
            pltpu.make_async_remote_copy(
                mine_anchor, anchors.at[par], anchor_sends.at[step], anchor_recvs.at[step], **to(cols, peer)
            )
        )
        copies.append(
            pltpu.make_async_remote_copy(mine, tiles.at[par], sends.at[step], recvs.at[step], **to(cols, peer))
        )
    for copy in copies:
        copy.start()
    for copy in copies:
        copy.wait()


def place_kernel(tiles, anchors, rows, placed):
    par = lax.axis_index("par")
    count = rows.shape[0] - 1

    def clear(i, carry):
        rows[i] = jnp.zeros(rows.shape[1:], F32)
        return carry

    lax.fori_loop(0, count + 1, clear, 0)
    for q in range(4):
        table = anchors[q]
        for t in range(2):
            first, shift = table[t, 0], table[t, 1]
            tile = tiles[q, t].reshape(48, 128)
            tile = jnp.concatenate([tile, jnp.zeros((48, CAP - 128), F32)], axis=1)
            tile = pltpu.roll(tile, shift, 1)
            for j in range(CAP // 128):
                placed[j] = tile[:, 128 * j : 128 * (j + 1)]
            for k in range(16):
                cols, owner = holder_of(first + k)
                spot = jnp.where(owner == par, cols, count)
                parts = [placed[j, pl.ds(k, 3, stride=16), :] for j in range(CAP // 128)]
                rows[spot] += jnp.concatenate(parts, axis=1)


def spread_kernel(rows, dip, spread, dip_out, send, recv, dip_send, dip_recv):
    cols, par = lax.axis_index("cols"), lax.axis_index("par")
    count = spread.shape[0]
    layer = layer_of(cols, par)
    mine = 4 * cols + par
    source_cols, source_par = layer // 4, layer % 4
    target_cols, target_par = holder_of(mine)
    same = (target_cols == cols) & (target_par == par)
    barrier = pltpu.get_barrier_semaphore()

    def greet(step, carry):
        pl.semaphore_signal(barrier, inc=1, **to((cols + step) % count, par))
        return carry

    lax.fori_loop(1, count, greet, 0)

    @pl.when(jnp.logical_not(same))
    def _():
        pl.semaphore_signal(barrier, inc=1, **to(source_cols, source_par))

    spread[cols] = rows[cols]
    pl.semaphore_wait(barrier, jnp.where(same, count - 1, count))

    def put(step, carry):
        peer = (cols + step) % count
        pltpu.make_async_remote_copy(rows.at[peer], spread.at[cols], send, recv, **to(peer, par)).start()
        return carry

    lax.fori_loop(1, count, put, 0)

    dip_copy = pltpu.make_async_remote_copy(dip, dip_out, dip_send, dip_recv, **to(target_cols, target_par))

    @pl.when(jnp.logical_not(same))
    def _():
        dip_copy.start()
        dip_copy.wait()

    @pl.when(same)
    def _():
        dip_out[...] = dip[...]

    others = spread.at[pl.ds(0, count - 1)]
    pltpu.make_async_copy(others, others, recv).wait()
    pltpu.make_async_copy(others, others, send).wait()


def lateral_kernel(bounds, spread, field, stage):
    count = spread.shape[0]
    params, rows_x, rows_y = field.shape

    def clear(i, carry):
        stage[:, pl.ds(pl.multiple_of(8 * i, 8), 8), :] = jnp.zeros((rows_y // 128, 8, 128), F32)
        return carry

    lax.fori_loop(0, stage.shape[1] // 8, clear, 0)

    def add(c, carry):
        start = bounds[c]
        row, shift = start // rows_y, start % rows_y
        part = jnp.concatenate([spread[c], jnp.zeros((8 - params, CAP), F32)], axis=0)
        part = jnp.concatenate([part, jnp.zeros((8, 3 * rows_y - CAP), F32)], axis=1)
        part = pltpu.roll(part, shift, 1)
        for k in range(3):
            spot = pl.ds(pl.multiple_of(8 * (row + k), 8), 8)
            for j in range(rows_y // 128):
                lane = k * rows_y + j * 128
                stage[j, spot, :] += part[:, lane : lane + 128]
        return carry

    lax.fori_loop(0, count, add, 0)
    for p in range(params):
        for k in range(rows_y // 128):
            field[p, :, pl.ds(k * 128, 128)] = stage[k, pl.ds(p, rows_x, stride=8), :]


def smooth_kernel(
    strength, couple, start, dip, out, fields, below, above, sends_up, recvs_up, sends_down, recvs_down, out_send, out_recv
):
    cols, par = lax.axis_index("cols"), lax.axis_index("par")
    params, rows_x, rows_y = start.shape
    layer = layer_of(cols, par)
    layers = 4 * lax.axis_size("cols")
    has_down, has_up = layer > 0, layer < layers - 1
    down_device = to(*holder_of(jnp.maximum(layer - 1, 0)))
    up_device = to(*holder_of(jnp.minimum(layer + 1, layers - 1)))
    target_cols, target_par = layer // 4, layer % 4
    source_cols, source_par = holder_of(4 * cols + par)
    same = (target_cols == cols) & (target_par == par)

    barrier = pltpu.get_barrier_semaphore()

    @pl.when(has_down)
    def _():
        pl.semaphore_signal(barrier, inc=1, **down_device)

    @pl.when(has_up)
    def _():
        pl.semaphore_signal(barrier, inc=1, **up_device)

    @pl.when(jnp.logical_not(same))
    def _():
        pl.semaphore_signal(barrier, inc=1, **to(source_cols, source_par))

    @pl.when(jnp.logical_not(has_down))
    def _():
        below[...] = jnp.zeros_like(below)

    @pl.when(jnp.logical_not(has_up))
    def _():
        above[...] = jnp.zeros_like(above)

    scale = []
    for p in range(params):
        row_sum = jnp.full((8, 128), couple[p, 0] + couple[p, 1] + couple[p, 2], F32)
        scale.append([(jnp.full((8, 128), couple[p, q], F32) / row_sum)[0, 0] for q in range(params)])

    tilt_x = dip[...] // 3 - 1
    tilt_y = dip[...] % 3 - 1
    at_x = lax.broadcasted_iota(jnp.int32, (rows_x, rows_y), 0)
    at_y = lax.broadcasted_iota(jnp.int32, (rows_x, rows_y), 1)

    pl.semaphore_wait(barrier, jnp.where(has_down, 1, 0) + jnp.where(has_up, 1, 0) + jnp.where(same, 0, 1))

    def pick(tilt, low, mid, high):
        return jnp.where(tilt < 0, low, jnp.where(tilt > 0, high, mid))

    for step in range(PASSES):
        slot = step % 2
        field = start if step == 0 else fields.at[slot]
        upward = pltpu.make_async_remote_copy(field, below.at[slot], sends_up.at[slot], recvs_up.at[slot], **up_device)
        downward = pltpu.make_async_remote_copy(field, above.at[slot], sends_down.at[slot], recvs_down.at[slot], **down_device)

        @pl.when(has_up)
        def _():
            upward.start()

        @pl.when(has_down)
        def _():
            downward.start()

        @pl.when(has_up)
        def _():
            upward.wait_send()
            downward.wait_recv()

        @pl.when(has_down)
        def _():
            downward.wait_send()
            upward.wait_recv()

        smooth = []
        for p in range(params):
            low, mid, high = below[slot, p], field[p], above[slot, p]
            rolled = lambda v, by, axis: pltpu.roll(v, by % v.shape[axis], axis)
            east = [rolled(v, -1, 0) for v in (low, mid, high)]
            west = [rolled(v, 1, 0) for v in (low, mid, high)]
            north = [rolled(v, -1, 1) for v in (low, mid, high)]
            south = [rolled(v, 1, 1) for v in (low, mid, high)]
            laplace = jnp.where(at_x < rows_x - 1, pick(tilt_x, *east), 0.0)
            laplace += jnp.where(at_x > 0, pick(tilt_x, *west[::-1]), 0.0)
            laplace += jnp.where(at_y < rows_y - 1, pick(tilt_y, *north), 0.0)
            laplace += jnp.where(at_y > 0, pick(tilt_y, *south[::-1]), 0.0)
            smooth.append(mid + strength[p] * (laplace - 4.0 * mid))
        for p in range(params):
            value = scale[p][0] * smooth[0] + scale[p][1] * smooth[1] + scale[p][2] * smooth[2]
            fields[1 - slot, p] = value

    last = fields.at[PASSES % 2]
    final = pltpu.make_async_remote_copy(last, out, out_send, out_recv, **to(target_cols, target_par))

    @pl.when(jnp.logical_not(same))
    def _():
        final.start()
        final.wait()

    @pl.when(same)
    def _():
        out[...] = last[...]


def shards(tile_bounds, tile_anchor, tile_picks, rmo_picks, sensitivity, dip_class, strength, couple):
    tile_count, ray_count, params, tile_z, tile_c = sensitivity.shape
    count = lax.axis_size("cols")
    _, rows_x, rows_y = dip_class.shape
    shape = jax.ShapeDtypeStruct
    dma = pltpu.SemaphoreType.DMA
    remote = lambda number: pltpu.CompilerParams(collective_id=number, has_side_effects=True)

    mine = pl.pallas_call(
        contribution_kernel,
        out_shape=shape((tile_count, params, tile_z, tile_c), F32),
        in_specs=[SMEM, VMEM, VMEM],
        out_specs=VMEM,
        name="contribution",
    )(tile_picks, rmo_picks, sensitivity)
    tiles, anchors = pl.pallas_call(
        share_kernel,
        out_shape=(shape((4, tile_count, params, tile_z, tile_c), F32), shape((4, 8, 128), jnp.int32)),
        in_specs=[SMEM, VMEM],
        out_specs=(VMEM, VMEM),
        scratch_shapes=[pltpu.VMEM((8, 128), jnp.int32), dma((3,)), dma((3,)), dma((3,)), dma((3,))],
        compiler_params=remote(0),
        name="share",
    )(tile_anchor, mine)
    rows = pl.pallas_call(
        place_kernel,
        out_shape=shape((count + 1, params, CAP), F32),
        in_specs=[VMEM, VMEM],
        out_specs=VMEM,
        scratch_shapes=[pltpu.VMEM((CAP // 128, params * tile_z, 128), F32)],
        name="place",
    )(tiles, anchors)
    spread, dip = pl.pallas_call(
        spread_kernel,
        out_shape=(shape((count, params, CAP), F32), shape((rows_x, rows_y), jnp.int32)),
        in_specs=[VMEM, VMEM],
        out_specs=(VMEM, VMEM),
        scratch_shapes=[dma, dma, dma, dma],
        compiler_params=remote(1),
        name="spread",
    )(rows, dip_class.reshape(rows_x, rows_y))
    start = pl.pallas_call(
        lateral_kernel,
        out_shape=shape((params, rows_x, rows_y), F32),
        in_specs=[SMEM, VMEM],
        out_specs=VMEM,
        scratch_shapes=[pltpu.VMEM((rows_y // 128, (rows_x + 3) * 8, 128), F32)],
        name="lateral",
    )(tile_bounds, spread)
    buffer = pltpu.VMEM((2, params, rows_x, rows_y), F32)
    field = pl.pallas_call(
        smooth_kernel,
        out_shape=shape((params, rows_x, rows_y), F32),
        in_specs=[SMEM, SMEM, VMEM, VMEM],
        out_specs=VMEM,
        scratch_shapes=[buffer, buffer, buffer, dma((2,)), dma((2,)), dma((2,)), dma((2,)), dma, dma],
        compiler_params=remote(2),
        name="smooth",
    )(strength, couple, start, dip)
    return field.reshape(params, 1, rows_x, rows_y)


def solution(mesh):
    return jax.shard_map(
        shards,
        mesh=mesh,
        in_specs=(
            P(),
            P(("cols", "par"), None),
            P(("cols", "par")),
            P(("cols", "par"), None),
            P(("cols", "par"), None, None, None, None),
            P(("cols", "par"), None, None),
            P(),
            P(),
        ),
        out_specs=P(None, ("cols", "par"), None, None),
        check_vma=False,
    )
```

```python
import jax
import jax.numpy as jnp
from jax import lax
from jax.experimental import pallas as pl
from jax.experimental.pallas import tpu as pltpu
from jax.sharding import PartitionSpec as P

CAP = 384
PASSES = 6
CHUNK = 8
F32 = jnp.float32
VMEM = pl.BlockSpec(memory_space=pltpu.VMEM)
SMEM = pl.BlockSpec(memory_space=pltpu.SMEM)


def layer_of(cols, par):
    plane, y_lo, x = cols // 8, (cols // 4) % 2, cols % 4
    y_hi, core = par // 2, par % 2
    place = 4 * (2 * y_hi + y_lo) + x + y_lo * (3 - 2 * x)
    place = place + (plane % 2) * (15 - 2 * place)
    return 32 * plane + 2 * place + core


def holder_of(layer):
    plane, rest = layer // 32, layer % 32
    place, core = rest // 2, rest % 2
    place = place + (plane % 2) * (15 - 2 * place)
    y, x = place // 4, place % 4
    y_lo = y % 2
    x = x + y_lo * (3 - 2 * x)
    return 8 * plane + 4 * y_lo + x, 2 * (y // 2) + core


def to(cols, par):
    return dict(device_id={"cols": cols, "par": par}, device_id_type=pl.DeviceIdType.MESH)


def step_kernel(
    bounds, anchor, picks, strength, couple, rmo, dip_in, sens_in, out,
    sens, tiles, placed, rows, spread, dip, table, rolled, stage, fields, below, above,
    sens_sem, share_send, share_recv, spread_send, spread_recv, dip_send, dip_recv,
    sends_up, recvs_up, sends_down, recvs_down, out_send, out_recv,
):
    cols, par = lax.axis_index("cols"), lax.axis_index("par")
    count = spread.shape[0]
    params, rows_x, rows_y = out.shape
    chunks = rows_x // CHUNK
    layer, layers = layer_of(cols, par), 4 * count
    has_down, has_up = layer > 0, layer < layers - 1
    down_device = to(*holder_of(jnp.maximum(layer - 1, 0)))
    up_device = to(*holder_of(jnp.minimum(layer + 1, layers - 1)))
    target_cols, target_par = layer // 4, layer % 4
    holder_cols, holder_par = holder_of(4 * cols + par)
    same = (target_cols == cols) & (target_par == par)
    other = jnp.logical_not(same)

    load = pltpu.make_async_copy(sens_in, sens, sens_sem)
    load.start()
    barrier = pltpu.get_barrier_semaphore()

    def greet(step, carry):
        pl.semaphore_signal(barrier, inc=1, **to((cols + step) % count, par))
        return carry

    lax.fori_loop(1, count, greet, 0)
    for step in (1, 2, 3):
        pl.semaphore_signal(barrier, inc=1, **to(cols, (par + step) % 4))

    @pl.when(has_down)
    def _():
        pl.semaphore_signal(barrier, inc=1, **down_device)

    @pl.when(has_up)
    def _():
        pl.semaphore_signal(barrier, inc=1, **up_device)

    @pl.when(other)
    def _():
        pl.semaphore_signal(barrier, inc=1, **to(target_cols, target_par))
        pl.semaphore_signal(barrier, inc=1, **to(holder_cols, holder_par))

    def find(line, seen):
        hit = jnp.where(bounds[seen] // 128 == line, 1, 0)
        table[line + 3] = jnp.where(hit == 1, seen, count)
        return seen + hit

    for k in range(3):
        table[k] = count
    lax.fori_loop(0, table.shape[0] - 3, find, 0)

    @pl.when(jnp.logical_not(has_down))
    def _():
        below[...] = jnp.zeros_like(below)

    @pl.when(jnp.logical_not(has_up))
    def _():
        above[...] = jnp.zeros_like(above)

    edge = jnp.zeros((2, params, 8, rows_y), F32)
    for ref in (fields, below, above):
        ref[:, :, pl.ds(0, 8), :] = edge
        ref[:, :, pl.ds(rows_x + 8, 8), :] = edge
    rolled[pl.ds(4 * count, 4)] = jnp.zeros((4, 8, 128), F32)

    scale = []
    for p in range(params):
        row_sum = jnp.full((8, 128), couple[p, 0] + couple[p, 1] + couple[p, 2], F32)
        scale.append([(jnp.full((8, 128), couple[p, q], F32) / row_sum)[0, 0] for q in range(params)])

    ray = lax.broadcasted_iota(jnp.int32, (1, rmo.shape[1]), 1)
    weights = [jnp.where(ray < picks[t], rmo[t : t + 1, :].astype(F32), 0.0) for t in range(2)]
    lane = lax.broadcasted_iota(jnp.int32, (48, 128), 1)
    row = lax.broadcasted_iota(jnp.int32, (8, 128), 0)
    load.wait()
    for t in range(2):
        total = jnp.zeros((params, 16, 128), F32)
        for r in range(rmo.shape[1]):
            total += weights[t][:, r : r + 1][None] * sens[t, r].astype(F32)
        tiles[0, pl.ds(48 * t, 48), :] = total.reshape(48, 128)
    facts = jnp.zeros((8, 128), F32)
    for k, value in enumerate((anchor[0, 0], anchor[1, 0], anchor[0, 1], anchor[1, 1])):
        facts = jnp.where(row == k, value.astype(F32), facts)
    tiles[0, pl.ds(96, 8), :] = facts

    remote_pairs = jnp.where(same, 0, 2)
    pl.semaphore_wait(barrier, count + 2 + remote_pairs + jnp.where(has_down, 1, 0) + jnp.where(has_up, 1, 0))

    shares = [
        pltpu.make_async_remote_copy(
            tiles.at[0], tiles.at[step], share_send.at[step - 1], share_recv.at[step - 1], **to(cols, (par + step) % 4)
        )
        for step in (1, 2, 3)
    ]
    for share in (shares[1], shares[2], shares[0]):
        share.start()
    dip_copy = pltpu.make_async_remote_copy(dip_in, dip, dip_send, dip_recv, **to(holder_cols, holder_par))

    @pl.when(other)
    def _():
        dip_copy.start()

    @pl.when(same)
    def _():
        dip[...] = dip_in[...]

    place = lax.broadcasted_iota(jnp.int32, (4 * count, 384), 0)
    item = lax.broadcasted_iota(jnp.int32, (4 * count, 384), 1)
    wanted = jnp.where(place % 4 == (item // 16) % 3, layer_of(place // 4, par) - item % 16, -1).astype(F32)
    item = lax.broadcasted_iota(jnp.int32, (1, 384), 1) // 48
    first = jnp.zeros((1, 384), F32)

    for slot in (0, 1, 2, 3):
        if slot:
            shares[slot - 1].wait()
        facts = tiles[slot, pl.ds(96, 8), :]
        wide = jnp.concatenate([facts] * 3, axis=1)
        for t in range(2):
            first = jnp.where(item == 2 * slot + t, wide[t : t + 1], first)
            shift = facts[2 + t, 0].astype(jnp.int32)
            fine, coarse = shift % 128, shift // 128
            tile = pltpu.roll(tiles[slot, pl.ds(48 * t, 48), :], fine, 1)
            keep = jnp.where(lane >= fine, tile, 0.0)
            wrap = tile - keep
            spot = pl.ds(96 * slot + 48 * t, 48)
            placed[spot, pl.ds(0, 128)] = jnp.where(coarse == 0, keep, 0.0)
            placed[spot, pl.ds(128, 128)] = jnp.where(coarse == 0, wrap, jnp.where(coarse == 1, keep, 0.0))
            placed[spot, pl.ds(256, 128)] = jnp.where(coarse == 2, keep, jnp.where(coarse == 1, wrap, 0.0))

    match = jnp.where(wanted == first, 1.0, 0.0).astype(jnp.bfloat16)
    value = placed[...]
    total = jnp.zeros((4 * count, CAP), F32)
    for _ in range(3):
        piece = value.astype(jnp.bfloat16)
        total += jnp.dot(match, piece, preferred_element_type=F32)
        value = value - piece.astype(F32)
    for c in range(count):
        rows[c] = total[4 * c : 4 * c + params]

    def put(i, carry):
        peer = (cols + (i + count // 2 - 1) % (count - 1) + 1) % count
        pltpu.make_async_remote_copy(rows.at[peer], spread.at[cols], spread_send, spread_recv, **to(peer, par)).start()
        return carry

    lax.fori_loop(0, count - 1, put, 0)
    spread[cols] = rows[cols]

    at_y = lax.broadcasted_iota(jnp.int32, (CHUNK, rows_y), 1)
    west_edge, east_edge = at_y == 0, at_y == rows_y - 1

    def chunk_of(c):
        return pl.ds(8 + CHUNK * c, CHUNK)

    def upward(slot, c):
        piece = (slot, slice(None), chunk_of(c))
        return pltpu.make_async_remote_copy(
            fields.at[piece], below.at[piece], sends_up.at[slot, c], recvs_up.at[slot, c], **up_device
        )

    def downward(slot, c):
        piece = (slot, slice(None), chunk_of(c))
        return pltpu.make_async_remote_copy(
            fields.at[piece], above.at[piece], sends_down.at[slot, c], recvs_down.at[slot, c], **down_device
        )

    def finish(c):
        return pltpu.make_async_remote_copy(
            fields.at[PASSES % 2, :, chunk_of(c)],
            out.at[:, pl.ds(CHUNK * c, CHUNK)],
            out_send,
            out_recv,
            **to(target_cols, target_par),
        )

    def send(slot, c):
        @pl.when(has_up)
        def _():
            upward(slot, c).start()

        @pl.when(has_down)
        def _():
            downward(slot, c).start()

    def receive(slot, c):
        @pl.when(has_down)
        def _():
            upward(slot, c).wait_recv()

        @pl.when(has_up)
        def _():
            downward(slot, c).wait_recv()

    def sent(slot, c):
        @pl.when(has_up)
        def _():
            upward(slot, c).wait_send()

        @pl.when(has_down)
        def _():
            downward(slot, c).wait_send()

    def pick(lower, higher, low, mid, high):
        return jnp.where(lower, low, jnp.where(higher, high, mid))

    others = spread.at[pl.ds(0, count - 1)]
    pltpu.make_async_copy(others, others, spread_recv).wait()

    lane = lax.broadcasted_iota(jnp.int32, (8, 128), 1)
    blank = jnp.zeros((8 - params, 128), F32)

    def turn(c, carry):
        fine = bounds[c] % 128
        before = jnp.zeros((8, 128), F32)
        for k in range(4):
            if k < 3:
                part = jnp.concatenate([spread[c, :, pl.ds(128 * k, 128)], blank], axis=0)
                part = pltpu.roll(part, fine, 1)
            else:
                part = jnp.zeros((8, 128), F32)
            rolled[4 * c + k] = jnp.where(lane >= fine, part, before)
            before = part
        return carry

    lax.fori_loop(0, count, turn, 0, unroll=4)
    for c in range(chunks):

        def gather(line, carry):
            total = rolled[4 * table[line + 3]]
            for k in range(1, 4):
                total += rolled[4 * table[line + 3 - k] + k]
            stage[pl.ds(pl.multiple_of(8 * line, 8), 8), :] = total
            return carry

        per_chunk = CHUNK * rows_y // 128
        lax.fori_loop(per_chunk * c, per_chunk * (c + 1), gather, 0, unroll=4)
        for p in range(params):
            for k in range(rows_y // 128):
                piece = stage[pl.ds(8 * per_chunk * c + 8 * k + p, CHUNK, stride=8 * rows_y // 128), :]
                fields[0, p, chunk_of(c), pl.ds(128 * k, 128)] = piece
        send(0, c)

    @pl.when(other)
    def _():
        dip_copy.wait()

    for step in range(PASSES):
        slot = step % 2
        for c in range(chunks):
            if c == 0:
                receive(slot, 0)
            if c + 1 < chunks:
                receive(slot, c + 1)
            if step > 0:
                sent(1 - slot, c)
            first = 8 + CHUNK * c
            kind = dip[pl.ds(CHUNK * c, CHUNK), :]
            across_low, across_high = kind < 3, kind >= 6
            along = kind - jnp.where(across_low, 0, jnp.where(across_high, 6, 3))
            along_low, along_high = along == 0, along == 2
            smooth = []
            for p in range(params):
                def rows(shift):
                    piece = (slot, p, pl.ds(first + shift, CHUNK))
                    return below[piece], fields[piece], above[piece]
                def rolled(values, by):
                    return [pltpu.roll(v, by % rows_y, 1) for v in values]
                here = rows(0)
                laplace = pick(across_low, across_high, *rows(1))
                laplace += pick(across_low, across_high, *rows(-1)[::-1])
                laplace += jnp.where(east_edge, 0.0, pick(along_low, along_high, *rolled(here, -1)))
                laplace += jnp.where(west_edge, 0.0, pick(along_low, along_high, *rolled(here, 1)[::-1]))
                smooth.append(here[1] + strength[p] * (laplace - 4.0 * here[1]))
            for p in range(params):
                value = scale[p][0] * smooth[0] + scale[p][1] * smooth[1] + scale[p][2] * smooth[2]
                fields[1 - slot, p, pl.ds(first, CHUNK), :] = value
                if step == PASSES - 1:
                    @pl.when(same)
                    def _():
                        out[p, pl.ds(CHUNK * c, CHUNK), :] = value
            if step < PASSES - 1:
                send(1 - slot, c)
            else:
                @pl.when(jnp.logical_not(same))
                def _():
                    finish(c).start()
    for c in range(chunks):
        sent(1 - PASSES % 2, c)

    @pl.when(jnp.logical_not(same))
    def _():
        pltpu.make_async_copy(out, out, out_recv).wait()
        pltpu.make_async_copy(out, out, out_send).wait()

    pltpu.make_async_copy(others, others, spread_send).wait()


def shards(tile_bounds, tile_anchor, tile_picks, rmo_picks, sensitivity, dip_class, strength, couple):
    tile_count, ray_count, params, tile_z, tile_c = sensitivity.shape
    count = lax.axis_size("cols")
    _, rows_x, rows_y = dip_class.shape
    dma = pltpu.SemaphoreType.DMA
    lines = rows_x * rows_y // 128
    buffer = pltpu.VMEM((2, params, rows_x + 16, rows_y), F32)
    message = pltpu.VMEM((count, params, CAP), F32)
    halo = dma((2, rows_x // CHUNK))
    field = pl.pallas_call(
        step_kernel,
        out_shape=jax.ShapeDtypeStruct((params, rows_x, rows_y), F32),
        in_specs=[SMEM, SMEM, SMEM, SMEM, SMEM, VMEM, VMEM, pl.BlockSpec(memory_space=pl.ANY)],
        out_specs=VMEM,
        scratch_shapes=[
            pltpu.VMEM(sensitivity.shape, sensitivity.dtype),
            pltpu.VMEM((4, 104, 128), F32),
            pltpu.VMEM((384, CAP), F32),
            message,
            message,
            pltpu.VMEM((rows_x, rows_y), jnp.int32),
            pltpu.SMEM((lines + 3,), jnp.int32),
            pltpu.VMEM((4 * count + 4, 8, 128), F32),
            pltpu.VMEM((8 * lines, 128), F32),
            buffer,
            buffer,
            buffer,
            dma,
            dma((3,)),
            dma((3,)),
            dma,
            dma,
            dma,
            dma,
            halo,
            halo,
            halo,
            halo,
            dma,
            dma,
        ],
        compiler_params=pltpu.CompilerParams(collective_id=0, has_side_effects=True),
        name="step",
    )(
        tile_bounds, tile_anchor, tile_picks, strength, couple, rmo_picks, dip_class.reshape(rows_x, rows_y), sensitivity
    )
    return field.reshape(params, 1, rows_x, rows_y)


def solution(mesh):
    return jax.shard_map(
        shards,
        mesh=mesh,
        in_specs=(
            P(),
            P(("cols", "par"), None),
            P(("cols", "par")),
            P(("cols", "par"), None),
            P(("cols", "par"), None, None, None, None),
            P(("cols", "par"), None, None),
            P(),
            P(),
        ),
        out_specs=P(None, ("cols", "par"), None, None),
        check_vma=False,
    )
```

```python
import jax
import jax.numpy as jnp
from jax import lax
from jax.experimental import pallas as pl
from jax.experimental.pallas import tpu as pltpu
from jax.sharding import PartitionSpec as P

CAP = 384
PASSES = 6
CHUNK = 8
F32 = jnp.float32
VMEM = pl.BlockSpec(memory_space=pltpu.VMEM)
SMEM = pl.BlockSpec(memory_space=pltpu.SMEM)


def layer_of(cols, par):
    plane, y_lo, x = cols // 8, (cols // 4) % 2, cols % 4
    y_hi, core = par // 2, par % 2
    place = 4 * (2 * y_hi + y_lo) + x + y_lo * (3 - 2 * x)
    place = place + (plane % 2) * (15 - 2 * place)
    return 32 * plane + 2 * place + core


def holder_of(layer):
    plane, rest = layer // 32, layer % 32
    place, core = rest // 2, rest % 2
    place = place + (plane % 2) * (15 - 2 * place)
    y, x = place // 4, place % 4
    y_lo = y % 2
    x = x + y_lo * (3 - 2 * x)
    return 8 * plane + 4 * y_lo + x, 2 * (y // 2) + core


def to(cols, par):
    return dict(device_id={"cols": cols, "par": par}, device_id_type=pl.DeviceIdType.MESH)


def step_kernel(
    bounds, anchor, picks, strength, couple, rmo, dip_in, sens_in, out,
    sens, tiles, placed, rows, spread, dip, table, rolled, stage, fields, below, above,
    ready, sens_sem, share_send, share_recv, spread_send, spread_recv, dip_send, dip_recv,
    sends_up, recvs_up, sends_down, recvs_down, out_send, out_recv,
):
    cols, par = lax.axis_index("cols"), lax.axis_index("par")
    count = lax.axis_size("cols")
    params, rows_x, rows_y = out.shape
    chunks = rows_x // CHUNK
    layer, layers = layer_of(cols, par), 4 * count
    has_down, has_up = layer > 0, layer < layers - 1
    down_device = to(*holder_of(jnp.maximum(layer - 1, 0)))
    up_device = to(*holder_of(jnp.minimum(layer + 1, layers - 1)))
    target_cols, target_par = layer // 4, layer % 4
    holder_cols, holder_par = holder_of(4 * cols + par)
    same = (target_cols == cols) & (target_par == par)
    other = jnp.logical_not(same)

    load = pltpu.make_async_copy(sens_in, sens, sens_sem)
    load.start()
    barrier = pltpu.get_barrier_semaphore()

    plane, spot = cols // 8, cols % 8
    planes = count // 8
    for step in range(1, planes):
        pl.semaphore_signal(barrier, inc=1, **to(8 * ((plane + step) % planes) + spot, par))
    for step in range(1, 8):
        pl.semaphore_signal(barrier, inc=1, **to(8 * plane + (spot + step) % 8, par))
    for step in (1, 2, 3):
        pl.semaphore_signal(barrier, inc=1, **to(cols, (par + step) % 4))

    @pl.when(has_down)
    def _():
        pl.semaphore_signal(barrier, inc=1, **down_device)

    @pl.when(has_up)
    def _():
        pl.semaphore_signal(barrier, inc=1, **up_device)

    @pl.when(other)
    def _():
        pl.semaphore_signal(barrier, inc=1, **to(target_cols, target_par))
        pl.semaphore_signal(barrier, inc=1, **to(holder_cols, holder_par))

    def find(line, seen):
        hit = jnp.where(bounds[seen] // 128 == line, 1, 0)
        table[line + 3] = jnp.where(hit == 1, seen, count)
        return seen + hit

    for k in range(3):
        table[k] = count
    lax.fori_loop(0, table.shape[0] - 3, find, 0)

    @pl.when(jnp.logical_not(has_down))
    def _():
        below[...] = jnp.zeros_like(below)

    @pl.when(jnp.logical_not(has_up))
    def _():
        above[...] = jnp.zeros_like(above)

    edge = jnp.zeros((2, params, 8, rows_y), F32)
    for ref in (fields, below, above):
        ref[:, :, pl.ds(0, 8), :] = edge
        ref[:, :, pl.ds(rows_x + 8, 8), :] = edge
    rolled[pl.ds(4 * count, 4)] = jnp.zeros((4, 8, 128), F32)

    scale = []
    for p in range(params):
        row_sum = jnp.full((8, 128), couple[p, 0] + couple[p, 1] + couple[p, 2], F32)
        scale.append([(jnp.full((8, 128), couple[p, q], F32) / row_sum)[0, 0] for q in range(params)])

    ray = lax.broadcasted_iota(jnp.int32, (1, rmo.shape[1]), 1)
    weights = [jnp.where(ray < picks[t], rmo[t : t + 1, :].astype(F32), 0.0) for t in range(2)]
    lane = lax.broadcasted_iota(jnp.int32, (48, 128), 1)
    row = lax.broadcasted_iota(jnp.int32, (8, 128), 0)
    load.wait()
    for t in range(2):
        total = jnp.zeros((params, 16, 128), F32)
        for r in range(rmo.shape[1]):
            total += weights[t][:, r : r + 1][None] * sens[t, r].astype(F32)
        tiles[0, pl.ds(48 * t, 48), :] = total.reshape(48, 128)
    facts = jnp.zeros((8, 128), F32)
    for k, value in enumerate((anchor[0, 0], anchor[1, 0], anchor[0, 1], anchor[1, 1])):
        facts = jnp.where(row == k, value.astype(F32), facts)
    tiles[0, pl.ds(96, 8), :] = facts

    remote_pairs = jnp.where(same, 0, 2)
    pl.semaphore_wait(barrier, planes + 9 + remote_pairs + jnp.where(has_down, 1, 0) + jnp.where(has_up, 1, 0))

    shares = [
        pltpu.make_async_remote_copy(
            tiles.at[0], tiles.at[step], share_send.at[step - 1], share_recv.at[step - 1], **to(cols, (par + step) % 4)
        )
        for step in (1, 2, 3)
    ]
    for share in (shares[1], shares[2], shares[0]):
        share.start()
    for step in range(1, planes):
        pl.semaphore_signal(ready, inc=1, **to(8 * ((plane + step) % planes) + spot, par))
    dip_copy = pltpu.make_async_remote_copy(dip_in, dip, dip_send, dip_recv, **to(holder_cols, holder_par))

    @pl.when(other)
    def _():
        dip_copy.start()

    @pl.when(same)
    def _():
        dip[...] = dip_in[...]

    place = lax.broadcasted_iota(jnp.int32, (4 * count, 384), 0)
    item = lax.broadcasted_iota(jnp.int32, (4 * count, 384), 1)
    wanted = jnp.where(place % 4 == (item // 16) % 3, layer_of(place // 4, par) - item % 16, -1).astype(F32)
    item = lax.broadcasted_iota(jnp.int32, (1, 384), 1) // 48
    first = jnp.zeros((1, 384), F32)

    for slot in (0, 1, 2, 3):
        if slot:
            shares[slot - 1].wait()
        facts = tiles[slot, pl.ds(96, 8), :]
        wide = jnp.concatenate([facts] * 3, axis=1)
        for t in range(2):
            first = jnp.where(item == 2 * slot + t, wide[t : t + 1], first)
            shift = facts[2 + t, 0].astype(jnp.int32)
            fine, coarse = shift % 128, shift // 128
            tile = pltpu.roll(tiles[slot, pl.ds(48 * t, 48), :], fine, 1)
            keep = jnp.where(lane >= fine, tile, 0.0)
            wrap = tile - keep
            spot = pl.ds(96 * slot + 48 * t, 48)
            placed[spot, pl.ds(0, 128)] = jnp.where(coarse == 0, keep, 0.0)
            placed[spot, pl.ds(128, 128)] = jnp.where(coarse == 0, wrap, jnp.where(coarse == 1, keep, 0.0))
            placed[spot, pl.ds(256, 128)] = jnp.where(coarse == 2, keep, jnp.where(coarse == 1, wrap, 0.0))

    match = jnp.where(wanted == first, 1.0, 0.0).astype(jnp.bfloat16)
    value = placed[...]
    total = jnp.zeros((4 * count, CAP), F32)
    for _ in range(3):
        piece = value.astype(jnp.bfloat16)
        total += jnp.dot(match, piece, preferred_element_type=F32)
        value = value - piece.astype(F32)
    for c in range(count):
        for k in range(3):
            rows[pl.ds(9 * c + 3 * k, 3), :] = total[4 * c : 4 * c + params, 128 * k : 128 * (k + 1)]

    pl.semaphore_wait(ready, planes - 1)

    def put(i, carry):
        step = (i % planes) * 8 + i // planes
        peer = (cols + step) % count
        pltpu.make_async_remote_copy(
            rows.at[pl.ds(9 * peer, 9)], spread.at[pl.ds(9 * cols, 9)], spread_send, spread_recv, **to(peer, par)
        ).start()
        return carry

    lax.fori_loop(1, count, put, 0)
    spread[pl.ds(9 * cols, 9)] = rows[pl.ds(9 * cols, 9)]

    at_y = lax.broadcasted_iota(jnp.int32, (CHUNK, rows_y), 1)
    west_edge, east_edge = at_y == 0, at_y == rows_y - 1

    def chunk_of(c):
        return pl.ds(8 + CHUNK * c, CHUNK)

    def upward(slot, c):
        piece = (slot, slice(None), chunk_of(c))
        return pltpu.make_async_remote_copy(
            fields.at[piece], below.at[piece], sends_up.at[slot, c], recvs_up.at[slot, c], **up_device
        )

    def downward(slot, c):
        piece = (slot, slice(None), chunk_of(c))
        return pltpu.make_async_remote_copy(
            fields.at[piece], above.at[piece], sends_down.at[slot, c], recvs_down.at[slot, c], **down_device
        )

    def finish(c):
        return pltpu.make_async_remote_copy(
            fields.at[PASSES % 2, :, chunk_of(c)],
            out.at[:, pl.ds(CHUNK * c, CHUNK)],
            out_send,
            out_recv,
            **to(target_cols, target_par),
        )

    def send(slot, c):
        @pl.when(has_up)
        def _():
            upward(slot, c).start()

        @pl.when(has_down)
        def _():
            downward(slot, c).start()

    def receive(slot, c):
        @pl.when(has_down)
        def _():
            upward(slot, c).wait_recv()

        @pl.when(has_up)
        def _():
            downward(slot, c).wait_recv()

    def sent(slot, c):
        @pl.when(has_up)
        def _():
            upward(slot, c).wait_send()

        @pl.when(has_down)
        def _():
            downward(slot, c).wait_send()

    def pick(lower, higher, low, mid, high):
        return jnp.where(lower, low, jnp.where(higher, high, mid))

    others = spread.at[pl.ds(0, 9 * (count - 1))]
    pltpu.make_async_copy(others, others, spread_recv).wait()

    lane = lax.broadcasted_iota(jnp.int32, (8, 128), 1)

    def turn(c, carry):
        fine = bounds[c] % 128
        before = jnp.zeros((8, 128), F32)
        for k in range(4):
            if k < 3:
                part = pltpu.roll(spread[pl.ds(9 * c + 3 * k, 8), :], fine, 1)
            else:
                part = jnp.zeros((8, 128), F32)
            rolled[4 * c + k] = jnp.where(lane >= fine, part, before)
            before = part
        return carry

    lax.fori_loop(0, count, turn, 0, unroll=4)
    for c in range(chunks):

        def gather(line, carry):
            total = rolled[4 * table[line + 3]]
            for k in range(1, 4):
                total += rolled[4 * table[line + 3 - k] + k]
            stage[pl.ds(pl.multiple_of(8 * line, 8), 8), :] = total
            return carry

        per_chunk = CHUNK * rows_y // 128
        lax.fori_loop(per_chunk * c, per_chunk * (c + 1), gather, 0, unroll=4)
        for p in range(params):
            for k in range(rows_y // 128):
                piece = stage[pl.ds(8 * per_chunk * c + 8 * k + p, CHUNK, stride=8 * rows_y // 128), :]
                fields[0, p, chunk_of(c), pl.ds(128 * k, 128)] = piece
        send(0, c)

    @pl.when(other)
    def _():
        dip_copy.wait()

    for step in range(PASSES):
        slot = step % 2
        for c in range(chunks):
            if c == 0:
                receive(slot, 0)
            if c + 1 < chunks:
                receive(slot, c + 1)
            if step > 0:
                sent(1 - slot, c)
            first = 8 + CHUNK * c
            kind = dip[pl.ds(CHUNK * c, CHUNK), :]
            across_low, across_high = kind < 3, kind >= 6
            along = kind - jnp.where(across_low, 0, jnp.where(across_high, 6, 3))
            along_low, along_high = along == 0, along == 2
            smooth = []
            for p in range(params):
                def rows(shift):
                    piece = (slot, p, pl.ds(first + shift, CHUNK))
                    return below[piece], fields[piece], above[piece]
                def rolled(values, by):
                    return [pltpu.roll(v, by % rows_y, 1) for v in values]
                here = rows(0)
                laplace = pick(across_low, across_high, *rows(1))
                laplace += pick(across_low, across_high, *rows(-1)[::-1])
                laplace += jnp.where(east_edge, 0.0, pick(along_low, along_high, *rolled(here, -1)))
                laplace += jnp.where(west_edge, 0.0, pick(along_low, along_high, *rolled(here, 1)[::-1]))
                smooth.append(here[1] + strength[p] * (laplace - 4.0 * here[1]))
            for p in range(params):
                value = scale[p][0] * smooth[0] + scale[p][1] * smooth[1] + scale[p][2] * smooth[2]
                fields[1 - slot, p, pl.ds(first, CHUNK), :] = value
                if step == PASSES - 1:
                    @pl.when(same)
                    def _():
                        out[p, pl.ds(CHUNK * c, CHUNK), :] = value
            if step < PASSES - 1:
                send(1 - slot, c)
            else:
                @pl.when(jnp.logical_not(same))
                def _():
                    finish(c).start()
    for c in range(chunks):
        sent(1 - PASSES % 2, c)

    @pl.when(jnp.logical_not(same))
    def _():
        pltpu.make_async_copy(out, out, out_recv).wait()
        pltpu.make_async_copy(out, out, out_send).wait()

    pltpu.make_async_copy(others, others, spread_send).wait()


def shards(tile_bounds, tile_anchor, tile_picks, rmo_picks, sensitivity, dip_class, strength, couple):
    tile_count, ray_count, params, tile_z, tile_c = sensitivity.shape
    count = lax.axis_size("cols")
    _, rows_x, rows_y = dip_class.shape
    dma = pltpu.SemaphoreType.DMA
    lines = rows_x * rows_y // 128
    buffer = pltpu.VMEM((2, params, rows_x + 16, rows_y), F32)
    message = pltpu.VMEM((9 * count + 8, 128), F32)
    halo = dma((2, rows_x // CHUNK))
    field = pl.pallas_call(
        step_kernel,
        out_shape=jax.ShapeDtypeStruct((params, rows_x, rows_y), F32),
        in_specs=[SMEM, SMEM, SMEM, SMEM, SMEM, VMEM, VMEM, pl.BlockSpec(memory_space=pl.ANY)],
        out_specs=VMEM,
        scratch_shapes=[
            pltpu.VMEM(sensitivity.shape, sensitivity.dtype),
            pltpu.VMEM((4, 104, 128), F32),
            pltpu.VMEM((384, CAP), F32),
            message,
            message,
            pltpu.VMEM((rows_x, rows_y), jnp.int32),
            pltpu.SMEM((lines + 3,), jnp.int32),
            pltpu.VMEM((4 * count + 4, 8, 128), F32),
            pltpu.VMEM((8 * lines, 128), F32),
            buffer,
            buffer,
            buffer,
            pltpu.SemaphoreType.REGULAR,
            dma,
            dma((3,)),
            dma((3,)),
            dma,
            dma,
            dma,
            dma,
            halo,
            halo,
            halo,
            halo,
            dma,
            dma,
        ],
        compiler_params=pltpu.CompilerParams(collective_id=0, has_side_effects=True),
        name="step",
    )(
        tile_bounds, tile_anchor, tile_picks, strength, couple, rmo_picks, dip_class.reshape(rows_x, rows_y), sensitivity
    )
    return field.reshape(params, 1, rows_x, rows_y)


def solution(mesh):
    return jax.shard_map(
        shards,
        mesh=mesh,
        in_specs=(
            P(),
            P(("cols", "par"), None),
            P(("cols", "par")),
            P(("cols", "par"), None),
            P(("cols", "par"), None, None, None, None),
            P(("cols", "par"), None, None),
            P(),
            P(),
        ),
        out_specs=P(None, ("cols", "par"), None, None),
        check_vma=False,
    )
```

```python
import jax
import jax.numpy as jnp
from jax import lax
from jax.experimental import pallas as pl
from jax.experimental.pallas import tpu as pltpu
from jax.sharding import PartitionSpec as P

CAP = 384
PASSES = 6
CHUNK = 8
F32 = jnp.float32
VMEM = pl.BlockSpec(memory_space=pltpu.VMEM)
SMEM = pl.BlockSpec(memory_space=pltpu.SMEM)


def layer_of(cols, par):
    plane, x = cols // 8, cols % 4
    y, core = 2 * (par // 2) + (cols // 4) % 2, par % 2
    middle, turn = ((y + 1) // 2) % 2, (y + 1) % 2
    place = 2 * x + (turn + x) % 2
    half = (middle + (place + 1) // 8) % 2
    return 32 * plane + 2 * (8 * half + place) + core


def holder_of(layer):
    plane, core = layer // 32, layer % 2
    half, place = (layer // 16) % 2, (layer // 2) % 8
    middle, turn = (half + (place + 1) // 8) % 2, ((place + 1) // 2) % 2
    y = (1 - middle) * 3 * (1 - turn) + middle * (1 + turn)
    return 8 * plane + 4 * (y % 2) + place // 2, 2 * (y // 2) + core


def to(cols, par):
    return dict(device_id={"cols": cols, "par": par}, device_id_type=pl.DeviceIdType.MESH)


def step_kernel(
    bounds, anchor, picks, strength, couple, rmo, dip_in, sens_in, out,
    sens, tiles, placed, rows, spread, dip, table, rolled, stage, fields, below, above,
    ready, sens_sem, share_send, share_recv, spread_send, spread_recv, dip_send, dip_recv,
    sends_up, recvs_up, sends_down, recvs_down, out_send, out_recv,
):
    cols, par = lax.axis_index("cols"), lax.axis_index("par")
    count = lax.axis_size("cols")
    params, rows_x, rows_y = out.shape
    chunks = rows_x // CHUNK
    layer, layers = layer_of(cols, par), 4 * count
    has_down, has_up = layer > 0, layer < layers - 1
    down_device = to(*holder_of(jnp.maximum(layer - 1, 0)))
    up_device = to(*holder_of(jnp.minimum(layer + 1, layers - 1)))
    target_cols, target_par = layer // 4, layer % 4
    holder_cols, holder_par = holder_of(4 * cols + par)
    same = (target_cols == cols) & (target_par == par)
    other = jnp.logical_not(same)

    load = pltpu.make_async_copy(sens_in, sens, sens_sem)
    load.start()
    barrier = pltpu.get_barrier_semaphore()

    plane, spot = cols // 8, cols % 8
    planes = count // 8
    for step in range(1, planes):
        pl.semaphore_signal(barrier, inc=1, **to(8 * ((plane + step) % planes) + spot, par))
    for step in range(1, 8):
        pl.semaphore_signal(barrier, inc=1, **to(8 * plane + (spot + step) % 8, par))
    for step in (1, 2, 3):
        pl.semaphore_signal(barrier, inc=1, **to(cols, (par + step) % 4))

    @pl.when(has_down)
    def _():
        pl.semaphore_signal(barrier, inc=1, **down_device)

    @pl.when(has_up)
    def _():
        pl.semaphore_signal(barrier, inc=1, **up_device)

    @pl.when(other)
    def _():
        pl.semaphore_signal(barrier, inc=1, **to(target_cols, target_par))
        pl.semaphore_signal(barrier, inc=1, **to(holder_cols, holder_par))

    def find(line, seen):
        hit = jnp.where(bounds[seen] // 128 == line, 1, 0)
        table[line + 3] = jnp.where(hit == 1, seen, count)
        return seen + hit

    for k in range(3):
        table[k] = count
    lax.fori_loop(0, table.shape[0] - 3, find, 0)

    @pl.when(jnp.logical_not(has_down))
    def _():
        below[...] = jnp.zeros_like(below)

    @pl.when(jnp.logical_not(has_up))
    def _():
        above[...] = jnp.zeros_like(above)

    edge = jnp.zeros((2, params, 8, rows_y), F32)
    for ref in (fields, below, above):
        ref[:, :, pl.ds(0, 8), :] = edge
        ref[:, :, pl.ds(rows_x + 8, 8), :] = edge
    rolled[pl.ds(4 * count, 4)] = jnp.zeros((4, 8, 128), F32)

    scale = []
    for p in range(params):
        row_sum = jnp.full((8, 128), couple[p, 0] + couple[p, 1] + couple[p, 2], F32)
        scale.append([(jnp.full((8, 128), couple[p, q], F32) / row_sum)[0, 0] for q in range(params)])

    ray = lax.broadcasted_iota(jnp.int32, (1, rmo.shape[1]), 1)
    weights = [jnp.where(ray < picks[t], rmo[t : t + 1, :].astype(F32), 0.0) for t in range(2)]
    lane = lax.broadcasted_iota(jnp.int32, (48, 128), 1)
    row = lax.broadcasted_iota(jnp.int32, (8, 128), 0)
    load.wait()
    for t in range(2):
        total = jnp.zeros((params, 16, 128), F32)
        for r in range(rmo.shape[1]):
            total += weights[t][:, r : r + 1][None] * sens[t, r].astype(F32)
        tiles[0, pl.ds(48 * t, 48), :] = total.reshape(48, 128)
    facts = jnp.zeros((8, 128), F32)
    for k, value in enumerate((anchor[0, 0], anchor[1, 0], anchor[0, 1], anchor[1, 1])):
        facts = jnp.where(row == k, value.astype(F32), facts)
    tiles[0, pl.ds(96, 8), :] = facts

    remote_pairs = jnp.where(same, 0, 2)
    pl.semaphore_wait(barrier, planes + 9 + remote_pairs + jnp.where(has_down, 1, 0) + jnp.where(has_up, 1, 0))

    shares = [
        pltpu.make_async_remote_copy(
            tiles.at[0], tiles.at[step], share_send.at[step - 1], share_recv.at[step - 1], **to(cols, (par + step) % 4)
        )
        for step in (1, 2, 3)
    ]
    for share in (shares[1], shares[2], shares[0]):
        share.start()
    for step in range(1, planes):
        pl.semaphore_signal(ready, inc=1, **to(8 * ((plane + step) % planes) + spot, par))
    dip_copy = pltpu.make_async_remote_copy(dip_in, dip, dip_send, dip_recv, **to(holder_cols, holder_par))

    place = lax.broadcasted_iota(jnp.int32, (4 * count, 384), 0)
    item = lax.broadcasted_iota(jnp.int32, (4 * count, 384), 1)
    wanted = jnp.where(place % 4 == (item // 16) % 3, layer_of(place // 4, par) - item % 16, -1).astype(F32)
    item = lax.broadcasted_iota(jnp.int32, (1, 384), 1) // 48
    first = jnp.zeros((1, 384), F32)

    for slot in (0, 1, 2, 3):
        if slot:
            shares[slot - 1].wait()
        facts = tiles[slot, pl.ds(96, 8), :]
        wide = jnp.concatenate([facts] * 3, axis=1)
        for t in range(2):
            first = jnp.where(item == 2 * slot + t, wide[t : t + 1], first)
            shift = facts[2 + t, 0].astype(jnp.int32)
            fine, coarse = shift % 128, shift // 128
            tile = pltpu.roll(tiles[slot, pl.ds(48 * t, 48), :], fine, 1)
            keep = jnp.where(lane >= fine, tile, 0.0)
            wrap = tile - keep
            spot = pl.ds(96 * slot + 48 * t, 48)
            placed[spot, pl.ds(0, 128)] = jnp.where(coarse == 0, keep, 0.0)
            placed[spot, pl.ds(128, 128)] = jnp.where(coarse == 0, wrap, jnp.where(coarse == 1, keep, 0.0))
            placed[spot, pl.ds(256, 128)] = jnp.where(coarse == 2, keep, jnp.where(coarse == 1, wrap, 0.0))

    match = jnp.where(wanted == first, 1.0, 0.0).astype(jnp.bfloat16)
    value = placed[...]
    total = jnp.zeros((4 * count, CAP), F32)
    for _ in range(3):
        piece = value.astype(jnp.bfloat16)
        total += jnp.dot(match, piece, preferred_element_type=F32)
        value = value - piece.astype(F32)
    for c in range(count):
        for k in range(3):
            rows[pl.ds(9 * c + 3 * k, 3), :] = total[4 * c : 4 * c + params, 128 * k : 128 * (k + 1)]

    pl.semaphore_wait(ready, planes - 1)

    def put(i, carry):
        step = (i % planes) * 8 + i // planes
        peer = (cols + step) % count
        pltpu.make_async_remote_copy(
            rows.at[pl.ds(9 * peer, 9)], spread.at[pl.ds(9 * cols, 9)], spread_send, spread_recv, **to(peer, par)
        ).start()
        return carry

    lax.fori_loop(1, count, put, 0)

    @pl.when(other)
    def _():
        dip_copy.start()

    @pl.when(same)
    def _():
        dip[...] = dip_in[...]

    spread[pl.ds(9 * cols, 9)] = rows[pl.ds(9 * cols, 9)]

    at_y = lax.broadcasted_iota(jnp.int32, (CHUNK, rows_y), 1)
    west_edge, east_edge = at_y == 0, at_y == rows_y - 1

    def chunk_of(c):
        return pl.ds(8 + CHUNK * c, CHUNK)

    def upward(slot, c):
        piece = (slot, slice(None), chunk_of(c))
        return pltpu.make_async_remote_copy(
            fields.at[piece], below.at[piece], sends_up.at[slot, c], recvs_up.at[slot, c], **up_device
        )

    def downward(slot, c):
        piece = (slot, slice(None), chunk_of(c))
        return pltpu.make_async_remote_copy(
            fields.at[piece], above.at[piece], sends_down.at[slot, c], recvs_down.at[slot, c], **down_device
        )

    def finish(c):
        return pltpu.make_async_remote_copy(
            fields.at[PASSES % 2, :, chunk_of(c)],
            out.at[:, pl.ds(CHUNK * c, CHUNK)],
            out_send,
            out_recv,
            **to(target_cols, target_par),
        )

    def send(slot, c):
        @pl.when(has_up)
        def _():
            upward(slot, c).start()

        @pl.when(has_down)
        def _():
            downward(slot, c).start()

    def receive(slot, c):
        @pl.when(has_down)
        def _():
            upward(slot, c).wait_recv()

        @pl.when(has_up)
        def _():
            downward(slot, c).wait_recv()

    def sent(slot, c):
        @pl.when(has_up)
        def _():
            upward(slot, c).wait_send()

        @pl.when(has_down)
        def _():
            downward(slot, c).wait_send()

    def pick(lower, higher, low, mid, high):
        return jnp.where(lower, low, jnp.where(higher, high, mid))

    others = spread.at[pl.ds(0, 9 * (count - 1))]
    pltpu.make_async_copy(others, others, spread_recv).wait()

    lane = lax.broadcasted_iota(jnp.int32, (8, 128), 1)

    def turn(c, carry):
        fine = bounds[c] % 128
        before = jnp.zeros((8, 128), F32)
        for k in range(4):
            if k < 3:
                part = pltpu.roll(spread[pl.ds(9 * c + 3 * k, 8), :], fine, 1)
            else:
                part = jnp.zeros((8, 128), F32)
            rolled[4 * c + k] = jnp.where(lane >= fine, part, before)
            before = part
        return carry

    lax.fori_loop(0, count, turn, 0, unroll=4)
    for c in range(chunks):

        def gather(line, carry):
            total = rolled[4 * table[line + 3]]
            for k in range(1, 4):
                total += rolled[4 * table[line + 3 - k] + k]
            stage[pl.ds(pl.multiple_of(8 * line, 8), 8), :] = total
            return carry

        per_chunk = CHUNK * rows_y // 128
        lax.fori_loop(per_chunk * c, per_chunk * (c + 1), gather, 0, unroll=4)
        for p in range(params):
            for k in range(rows_y // 128):
                piece = stage[pl.ds(8 * per_chunk * c + 8 * k + p, CHUNK, stride=8 * rows_y // 128), :]
                fields[0, p, chunk_of(c), pl.ds(128 * k, 128)] = piece
        send(0, c)

    @pl.when(other)
    def _():
        dip_copy.wait()

    for step in range(PASSES):
        slot = step % 2
        for c in range(chunks):
            if c == 0:
                receive(slot, 0)
            if c + 1 < chunks:
                receive(slot, c + 1)
            if step > 0:
                sent(1 - slot, c)
            first = 8 + CHUNK * c
            kind = dip[pl.ds(CHUNK * c, CHUNK), :]
            across_low, across_high = kind < 3, kind >= 6
            along = kind - jnp.where(across_low, 0, jnp.where(across_high, 6, 3))
            along_low, along_high = along == 0, along == 2
            smooth = []
            for p in range(params):
                def rows(shift):
                    piece = (slot, p, pl.ds(first + shift, CHUNK))
                    return below[piece], fields[piece], above[piece]
                def rolled(values, by):
                    return [pltpu.roll(v, by % rows_y, 1) for v in values]
                here = rows(0)
                laplace = pick(across_low, across_high, *rows(1))
                laplace += pick(across_low, across_high, *rows(-1)[::-1])
                laplace += jnp.where(east_edge, 0.0, pick(along_low, along_high, *rolled(here, -1)))
                laplace += jnp.where(west_edge, 0.0, pick(along_low, along_high, *rolled(here, 1)[::-1]))
                smooth.append(here[1] + strength[p] * (laplace - 4.0 * here[1]))
            for p in range(params):
                value = scale[p][0] * smooth[0] + scale[p][1] * smooth[1] + scale[p][2] * smooth[2]
                fields[1 - slot, p, pl.ds(first, CHUNK), :] = value
                if step == PASSES - 1:
                    @pl.when(same)
                    def _():
                        out[p, pl.ds(CHUNK * c, CHUNK), :] = value
            if step < PASSES - 1:
                send(1 - slot, c)
            else:
                @pl.when(jnp.logical_not(same))
                def _():
                    finish(c).start()
    for c in range(chunks):
        sent(1 - PASSES % 2, c)

    @pl.when(jnp.logical_not(same))
    def _():
        pltpu.make_async_copy(out, out, out_recv).wait()
        pltpu.make_async_copy(out, out, out_send).wait()

    pltpu.make_async_copy(others, others, spread_send).wait()


def shards(tile_bounds, tile_anchor, tile_picks, rmo_picks, sensitivity, dip_class, strength, couple):
    tile_count, ray_count, params, tile_z, tile_c = sensitivity.shape
    count = lax.axis_size("cols")
    _, rows_x, rows_y = dip_class.shape
    dma = pltpu.SemaphoreType.DMA
    lines = rows_x * rows_y // 128
    buffer = pltpu.VMEM((2, params, rows_x + 16, rows_y), F32)
    message = pltpu.VMEM((9 * count + 8, 128), F32)
    halo = dma((2, rows_x // CHUNK))
    field = pl.pallas_call(
        step_kernel,
        out_shape=jax.ShapeDtypeStruct((params, rows_x, rows_y), F32),
        in_specs=[SMEM, SMEM, SMEM, SMEM, SMEM, VMEM, VMEM, pl.BlockSpec(memory_space=pl.ANY)],
        out_specs=VMEM,
        scratch_shapes=[
            pltpu.VMEM(sensitivity.shape, sensitivity.dtype),
            pltpu.VMEM((4, 104, 128), F32),
            pltpu.VMEM((384, CAP), F32),
            message,
            message,
            pltpu.VMEM((rows_x, rows_y), jnp.int32),
            pltpu.SMEM((lines + 3,), jnp.int32),
            pltpu.VMEM((4 * count + 4, 8, 128), F32),
            pltpu.VMEM((8 * lines, 128), F32),
            buffer,
            buffer,
            buffer,
            pltpu.SemaphoreType.REGULAR,
            dma,
            dma((3,)),
            dma((3,)),
            dma,
            dma,
            dma,
            dma,
            halo,
            halo,
            halo,
            halo,
            dma,
            dma,
        ],
        compiler_params=pltpu.CompilerParams(collective_id=0, has_side_effects=True),
        name="step",
    )(
        tile_bounds, tile_anchor, tile_picks, strength, couple, rmo_picks, dip_class.reshape(rows_x, rows_y), sensitivity
    )
    return field.reshape(params, 1, rows_x, rows_y)


def solution(mesh):
    return jax.shard_map(
        shards,
        mesh=mesh,
        in_specs=(
            P(),
            P(("cols", "par"), None),
            P(("cols", "par")),
            P(("cols", "par"), None),
            P(("cols", "par"), None, None, None, None),
            P(("cols", "par"), None, None),
            P(),
            P(),
        ),
        out_specs=P(None, ("cols", "par"), None, None),
        check_vma=False,
    )
```

```python
import jax
import jax.numpy as jnp
from jax import lax
from jax.experimental import pallas as pl
from jax.experimental.pallas import tpu as pltpu
from jax.sharding import PartitionSpec as P

CAP = 384
PASSES = 6
CHUNK = 8
F32 = jnp.float32
VMEM = pl.BlockSpec(memory_space=pltpu.VMEM)
SMEM = pl.BlockSpec(memory_space=pltpu.SMEM)


def layer_of(cols, par):
    plane, x = cols // 8, cols % 4
    y, core = 2 * (par // 2) + (cols // 4) % 2, par % 2
    middle, turn = ((y + 1) // 2) % 2, (y + 1) % 2
    place = 2 * x + (turn + x) % 2
    half = (middle + (place + 1) // 8) % 2
    return 32 * plane + 2 * (8 * half + place) + core


def holder_of(layer):
    plane, core = layer // 32, layer % 2
    half, place = (layer // 16) % 2, (layer // 2) % 8
    middle, turn = (half + (place + 1) // 8) % 2, ((place + 1) // 2) % 2
    y = (1 - middle) * 3 * (1 - turn) + middle * (1 + turn)
    return 8 * plane + 4 * (y % 2) + place // 2, 2 * (y // 2) + core


def to(cols, par):
    return dict(device_id={"cols": cols, "par": par}, device_id_type=pl.DeviceIdType.MESH)


def step_kernel(
    bounds, anchor, picks, strength, couple, rmo, dip_in, sens_in, out,
    sens, tiles, placed, rows, spread, dip, table, rolled, stage, fields, below, above,
    ready, sens_sem, share_send, share_recv, spread_send, spread_recv, dip_send, dip_recv,
    sends_up, recvs_up, sends_down, recvs_down, out_send, out_recv,
):
    cols, par = lax.axis_index("cols"), lax.axis_index("par")
    count = lax.axis_size("cols")
    params, rows_x, rows_y = out.shape
    chunks = rows_x // CHUNK
    layer, layers = layer_of(cols, par), 4 * count
    has_down, has_up = layer > 0, layer < layers - 1
    down_device = to(*holder_of(jnp.maximum(layer - 1, 0)))
    up_device = to(*holder_of(jnp.minimum(layer + 1, layers - 1)))
    target_cols, target_par = layer // 4, layer % 4
    holder_cols, holder_par = holder_of(4 * cols + par)
    same = (target_cols == cols) & (target_par == par)
    other = jnp.logical_not(same)

    load = pltpu.make_async_copy(sens_in, sens, sens_sem)
    load.start()
    barrier = pltpu.get_barrier_semaphore()

    plane, spot = cols // 8, cols % 8
    planes = count // 8
    for step in range(1, planes):
        pl.semaphore_signal(barrier, inc=1, **to(8 * ((plane + step) % planes) + spot, par))
    for step in range(1, 8):
        pl.semaphore_signal(barrier, inc=1, **to(8 * plane + (spot + step) % 8, par))
    for step in (1, 2, 3):
        pl.semaphore_signal(barrier, inc=1, **to(cols, (par + step) % 4))

    @pl.when(has_down)
    def _():
        pl.semaphore_signal(barrier, inc=1, **down_device)

    @pl.when(has_up)
    def _():
        pl.semaphore_signal(barrier, inc=1, **up_device)

    @pl.when(other)
    def _():
        pl.semaphore_signal(barrier, inc=1, **to(target_cols, target_par))
        pl.semaphore_signal(barrier, inc=1, **to(holder_cols, holder_par))

    def find(line, seen):
        hit = jnp.where(bounds[seen] // 128 == line, 1, 0)
        table[line + 3] = jnp.where(hit == 1, seen, count)
        return seen + hit

    for k in range(3):
        table[k] = count
    lax.fori_loop(0, table.shape[0] - 3, find, 0)

    @pl.when(jnp.logical_not(has_down))
    def _():
        below[...] = jnp.zeros_like(below)

    @pl.when(jnp.logical_not(has_up))
    def _():
        above[...] = jnp.zeros_like(above)

    edge = jnp.zeros((2, params, 8, rows_y), F32)
    for ref in (fields, below, above):
        ref[:, :, pl.ds(0, 8), :] = edge
        ref[:, :, pl.ds(rows_x + 8, 8), :] = edge
    rolled[pl.ds(4 * count, 4)] = jnp.zeros((4, 8, 128), F32)

    scale = []
    for p in range(params):
        row_sum = jnp.full((8, 128), couple[p, 0] + couple[p, 1] + couple[p, 2], F32)
        scale.append([(jnp.full((8, 128), couple[p, q], F32) / row_sum)[0, 0] for q in range(params)])

    ray = lax.broadcasted_iota(jnp.int32, (1, rmo.shape[1]), 1)
    weights = [jnp.where(ray < picks[t], rmo[t : t + 1, :].astype(F32), 0.0) for t in range(2)]
    lane = lax.broadcasted_iota(jnp.int32, (48, 128), 1)
    row = lax.broadcasted_iota(jnp.int32, (8, 128), 0)
    load.wait()
    for t in range(2):
        total = jnp.zeros((params, 16, 128), F32)
        for r in range(rmo.shape[1]):
            total += weights[t][:, r : r + 1][None] * sens[t, r].astype(F32)
        tiles[0, pl.ds(48 * t, 48), :] = total.reshape(48, 128)
    facts = jnp.zeros((8, 128), F32)
    for k, value in enumerate((anchor[0, 0], anchor[1, 0], anchor[0, 1], anchor[1, 1])):
        facts = jnp.where(row == k, value.astype(F32), facts)
    tiles[0, pl.ds(96, 8), :] = facts

    remote_pairs = jnp.where(same, 0, 2)
    pl.semaphore_wait(barrier, planes + 9 + remote_pairs + jnp.where(has_down, 1, 0) + jnp.where(has_up, 1, 0))

    shares = [
        pltpu.make_async_remote_copy(
            tiles.at[0], tiles.at[step], share_send.at[step - 1], share_recv.at[step - 1], **to(cols, (par + step) % 4)
        )
        for step in (1, 2, 3)
    ]
    for share in (shares[1], shares[2], shares[0]):
        share.start()
    for step in range(1, planes):
        pl.semaphore_signal(ready, inc=1, **to(8 * ((plane + step) % planes) + spot, par))
    dip_copy = pltpu.make_async_remote_copy(dip_in, dip, dip_send, dip_recv, **to(holder_cols, holder_par))

    place = lax.broadcasted_iota(jnp.int32, (4 * count, 384), 0)
    item = lax.broadcasted_iota(jnp.int32, (4 * count, 384), 1)
    wanted = jnp.where(place % 4 == (item // 16) % 3, layer_of(place // 4, par) - item % 16, -1).astype(F32)
    item = lax.broadcasted_iota(jnp.int32, (1, 384), 1) // 48
    first = jnp.zeros((1, 384), F32)

    for slot in (0, 1, 2, 3):
        if slot:
            shares[slot - 1].wait()
        facts = tiles[slot, pl.ds(96, 8), :]
        wide = jnp.concatenate([facts] * 3, axis=1)
        for t in range(2):
            first = jnp.where(item == 2 * slot + t, wide[t : t + 1], first)
            shift = facts[2 + t, 0].astype(jnp.int32)
            fine, coarse = shift % 128, shift // 128
            tile = pltpu.roll(tiles[slot, pl.ds(48 * t, 48), :], fine, 1)
            keep = jnp.where(lane >= fine, tile, 0.0)
            wrap = tile - keep
            spot = pl.ds(96 * slot + 48 * t, 48)
            placed[spot, pl.ds(0, 128)] = jnp.where(coarse == 0, keep, 0.0)
            placed[spot, pl.ds(128, 128)] = jnp.where(coarse == 0, wrap, jnp.where(coarse == 1, keep, 0.0))
            placed[spot, pl.ds(256, 128)] = jnp.where(coarse == 2, keep, jnp.where(coarse == 1, wrap, 0.0))

    match = jnp.where(wanted == first, 1.0, 0.0).astype(jnp.bfloat16)
    value = placed[...]
    total = jnp.zeros((4 * count, CAP), F32)
    for _ in range(3):
        piece = value.astype(jnp.bfloat16)
        total += jnp.dot(match, piece, preferred_element_type=F32)
        value = value - piece.astype(F32)
    for c in range(count):
        for k in range(3):
            rows[pl.ds(9 * c + 3 * k, 3), :] = total[4 * c : 4 * c + params, 128 * k : 128 * (k + 1)]

    pl.semaphore_wait(ready, planes - 1)

    def put(i, carry):
        step = (i % planes) * 8 + i // planes
        peer = (cols + step) % count
        pltpu.make_async_remote_copy(
            rows.at[pl.ds(9 * peer, 9)], spread.at[pl.ds(9 * cols, 9)], spread_send, spread_recv, **to(peer, par)
        ).start()
        return carry

    lax.fori_loop(1, count, put, 0)

    @pl.when(other)
    def _():
        dip_copy.start()

    @pl.when(same)
    def _():
        dip[...] = dip_in[...]

    spread[pl.ds(9 * cols, 9)] = rows[pl.ds(9 * cols, 9)]

    at_y = lax.broadcasted_iota(jnp.int32, (CHUNK, rows_y), 1)
    west_edge, east_edge = at_y == 0, at_y == rows_y - 1

    def chunk_of(c):
        return pl.ds(8 + CHUNK * c, CHUNK)

    def upward(slot, c):
        piece = (slot, slice(None), chunk_of(c))
        return pltpu.make_async_remote_copy(
            fields.at[piece], below.at[piece], sends_up.at[slot, c], recvs_up.at[slot, c], **up_device
        )

    def downward(slot, c):
        piece = (slot, slice(None), chunk_of(c))
        return pltpu.make_async_remote_copy(
            fields.at[piece], above.at[piece], sends_down.at[slot, c], recvs_down.at[slot, c], **down_device
        )

    def finish(c):
        return pltpu.make_async_remote_copy(
            fields.at[PASSES % 2, :, chunk_of(c)],
            out.at[:, pl.ds(CHUNK * c, CHUNK)],
            out_send,
            out_recv,
            **to(target_cols, target_par),
        )

    def send(slot, c):
        @pl.when(has_up)
        def _():
            upward(slot, c).start()

        @pl.when(has_down)
        def _():
            downward(slot, c).start()

    def receive(slot, c):
        @pl.when(has_down)
        def _():
            upward(slot, c).wait_recv()

        @pl.when(has_up)
        def _():
            downward(slot, c).wait_recv()

    def sent(slot, c):
        @pl.when(has_up)
        def _():
            upward(slot, c).wait_send()

        @pl.when(has_down)
        def _():
            downward(slot, c).wait_send()

    def pick(lower, higher, low, mid, high):
        return jnp.where(lower, low, jnp.where(higher, high, mid))

    others = spread.at[pl.ds(0, 9 * (count - 1))]
    pltpu.make_async_copy(others, others, spread_recv).wait()

    lane = lax.broadcasted_iota(jnp.int32, (8, 128), 1)

    def turn(c, carry):
        fine = bounds[c] % 128
        before = jnp.zeros((8, 128), F32)
        for k in range(4):
            if k < 3:
                part = pltpu.roll(spread[pl.ds(9 * c + 3 * k, 8), :], fine, 1)
            else:
                part = jnp.zeros((8, 128), F32)
            rolled[4 * c + k] = jnp.where(lane >= fine, part, before)
            before = part
        return carry

    lax.fori_loop(0, count, turn, 0, unroll=4)
    for c in range(chunks):

        def gather(line, carry):
            total = rolled[4 * table[line + 3]]
            for k in range(1, 4):
                total += rolled[4 * table[line + 3 - k] + k]
            stage[pl.ds(pl.multiple_of(8 * line, 8), 8), :] = total
            return carry

        per_chunk = CHUNK * rows_y // 128
        lax.fori_loop(per_chunk * c, per_chunk * (c + 1), gather, 0, unroll=4)
        for p in range(params):
            for k in range(rows_y // 128):
                piece = stage[pl.ds(8 * per_chunk * c + 8 * k + p, CHUNK, stride=8 * rows_y // 128), :]
                fields[0, p, chunk_of(c), pl.ds(128 * k, 128)] = piece
        send(0, c)

    @pl.when(other)
    def _():
        dip_copy.wait()

    for step in range(PASSES):
        slot = step % 2
        for c in range(chunks):
            if c == 0:
                receive(slot, 0)
            if c + 1 < chunks:
                receive(slot, c + 1)
            if step > 0:
                sent(1 - slot, c)
            first = 8 + CHUNK * c
            kind = dip[pl.ds(CHUNK * c, CHUNK), :]
            across_low, across_high = kind < 3, kind >= 6
            along = kind - jnp.where(across_low, 0, jnp.where(across_high, 6, 3))
            along_low, along_high = along == 0, along == 2
            smooth = []
            for p in range(params):
                def rows(shift):
                    piece = (slot, p, pl.ds(first + shift, CHUNK))
                    return below[piece], fields[piece], above[piece]
                def rolled(values, by):
                    return [pltpu.roll(v, by % rows_y, 1) for v in values]
                here = rows(0)
                laplace = pick(across_low, across_high, *rows(1))
                laplace += pick(across_low, across_high, *rows(-1)[::-1])
                laplace += jnp.where(east_edge, 0.0, pick(along_low, along_high, *rolled(here, -1)))
                laplace += jnp.where(west_edge, 0.0, pick(along_low, along_high, *rolled(here, 1)[::-1]))
                smooth.append(here[1] + strength[p] * (laplace - 4.0 * here[1]))
            for p in range(params):
                value = scale[p][0] * smooth[0] + scale[p][1] * smooth[1] + scale[p][2] * smooth[2]
                fields[1 - slot, p, pl.ds(first, CHUNK), :] = value
                if step == PASSES - 1:
                    @pl.when(same)
                    def _():
                        out[p, pl.ds(CHUNK * c, CHUNK), :] = value
            if step < PASSES - 1:
                send(1 - slot, c)
            else:
                @pl.when(jnp.logical_not(same))
                def _():
                    finish(c).start()
    for c in range(chunks):
        sent(1 - PASSES % 2, c)

    @pl.when(jnp.logical_not(same))
    def _():
        pltpu.make_async_copy(out, out, out_recv).wait()
        pltpu.make_async_copy(out, out, out_send).wait()

    pltpu.make_async_copy(others, others, spread_send).wait()


def shards(tile_bounds, tile_anchor, tile_picks, rmo_picks, sensitivity, dip_class, strength, couple):
    tile_count, ray_count, params, tile_z, tile_c = sensitivity.shape
    count = lax.axis_size("cols")
    _, rows_x, rows_y = dip_class.shape
    dma = pltpu.SemaphoreType.DMA
    lines = rows_x * rows_y // 128
    buffer = pltpu.VMEM((2, params, rows_x + 16, rows_y), F32)
    message = pltpu.VMEM((9 * count + 8, 128), F32)
    halo = dma((2, rows_x // CHUNK))
    field = pl.pallas_call(
        step_kernel,
        out_shape=pltpu.VMEM((params, rows_x, rows_y), F32),
        in_specs=[SMEM, SMEM, SMEM, SMEM, SMEM, VMEM, VMEM, pl.BlockSpec(memory_space=pl.ANY)],
        out_specs=VMEM,
        scratch_shapes=[
            pltpu.VMEM(sensitivity.shape, sensitivity.dtype),
            pltpu.VMEM((4, 104, 128), F32),
            pltpu.VMEM((384, CAP), F32),
            message,
            message,
            pltpu.VMEM((rows_x, rows_y), jnp.int32),
            pltpu.SMEM((lines + 3,), jnp.int32),
            pltpu.VMEM((4 * count + 4, 8, 128), F32),
            pltpu.VMEM((8 * lines, 128), F32),
            buffer,
            buffer,
            buffer,
            pltpu.SemaphoreType.REGULAR,
            dma,
            dma((3,)),
            dma((3,)),
            dma,
            dma,
            dma,
            dma,
            halo,
            halo,
            halo,
            halo,
            dma,
            dma,
        ],
        compiler_params=pltpu.CompilerParams(collective_id=0, has_side_effects=True),
        name="step",
    )(
        tile_bounds, tile_anchor, tile_picks, strength, couple, rmo_picks, dip_class.reshape(rows_x, rows_y), sensitivity
    )
    return field.reshape(params, 1, rows_x, rows_y)


def solution(mesh):
    return jax.shard_map(
        shards,
        mesh=mesh,
        in_specs=(
            P(),
            P(("cols", "par"), None),
            P(("cols", "par")),
            P(("cols", "par"), None),
            P(("cols", "par"), None, None, None, None),
            P(("cols", "par"), None, None),
            P(),
            P(),
        ),
        out_specs=P(None, ("cols", "par"), None, None),
        check_vma=False,
    )
```
